256 devices in a mesh: gx: 4 (over x_lo, core), gy: 16 (over x_hi, z), gz: 4 (over y).
Axes of the slice: x: 4 (x_hi: 2, x_lo: 2; x = x_hi * 2 + x_lo), y: 4, z: 8, core: 2. Of those that a mesh axis runs over, the one named last changes fastest.
Arguments:
- field: bfloat16 [64, 8, 384, 1536], P(None, 'gz', 'gy', 'gx'), may hold values from -200 to 200, as said below
- mode_one_factor: bfloat16 [1536, 256], P('gx'), may hold values from -0.15625 to 0.15625
- mode_two_factor: bfloat16 [384, 256], P('gy'), may hold values from -0.3125 to 0.3125
Outputs:
- gram_one: float32 [1536, 1536], P('gx')
- gram_two: float32 [384, 384], P('gy')
- core: bfloat16 [64, 8, 256, 256], P('gx', 'gz', 'gy')
The draws below stay inside these ranges and needn't reach their ends.
Inputs may be any that keep to these rules, and one draw needn't show every extreme that they name: `field`: the snapshot's values lie within -200 and 200.
All inputs are finite; a program needn't handle non-finite values.
Results may differ from the reference program's by a relative error of at most 0.005.
Values may be sent and summed in bfloat16 or wider, within the bound.
A program may use at most 128 MiB of HBM per device.

```python
import jax
import jax.numpy as jnp
from jax import lax

V = 64
R1 = 256
R2 = 256
N2 = 384
N1 = 1536
N3 = 8


def draw_field(key, part):
    keys = jax.random.split(jax.random.fold_in(key, 7), 6)
    shape_full = (V, N3, N2, N1)
    noise = jnp.clip(jax.random.normal(keys[0], shape_full, jnp.float32), -4.0, 4.0)
    row_scale = jnp.exp(jax.random.uniform(keys[1], (1, 1, 1, N1), jnp.float32, jnp.log(0.5), jnp.log(5.0)))
    mixing = 0.1
    common = jnp.clip(jax.random.normal(keys[2], (V, N3, N2, 1), jnp.float32), -4.0, 4.0)
    pattern = jnp.clip(jax.random.normal(keys[3], (1, 1, 1, N1), jnp.float32) * mixing, -1.5, 1.5)
    var_scale = jnp.exp(jax.random.uniform(keys[4], (V, 1, 1, 1), jnp.float32, jnp.log(0.5), jnp.log(2.0)))
    col_scale = jnp.exp(jax.random.uniform(keys[5], (1, 1, N2, 1), jnp.float32, jnp.log(0.5), jnp.log(2.0)))
    values = row_scale * var_scale * col_scale * (noise + pattern * common)
    return values.astype(jnp.bfloat16)


def level_of(own_key, dims, pieces, smallest, top_value):
    def one(dim, blocks):
        steps = jax.random.uniform(jax.random.fold_in(jax.random.fold_in(own_key, 6), dim), (blocks,), jnp.float32, smallest / len(pieces), top_value / len(pieces))
        return jnp.repeat(jnp.exp(steps), dims[dim] // blocks).reshape((-1,) + (1,) * (len(dims) - dim - 1))

    factor_of = one(*pieces[0])
    for cut in pieces[1:]:
        factor_of = factor_of * one(*cut)
    return factor_of


def centred(key, extent, spread, bound, cuts=(), dtype=jnp.bfloat16):
    entries = spread * jax.random.normal(key, extent, jnp.float32)
    if cuts:
        entries = entries * level_of(key, extent, cuts, -0.22, 0.18)
    return jnp.clip(entries, -bound, bound).astype(dtype)


def setup_inputs(seed: int = 0) -> dict:
    key_of = jax.random.split(jax.random.key(seed), 4)
    field = draw_field(jax.random.fold_in(key_of[3], 71), 0)
    mode_one_factor = centred(key_of[1], (N1, R1), N1 ** -0.5, 0.15625, ((0, 4),))
    mode_two_factor = centred(key_of[2], (N2, R2), N2 ** -0.5, 0.3125, ((0, 16),))
    return {"field": field, "mode_one_factor": mode_one_factor, "mode_two_factor": mode_two_factor}


def reference(field, mode_one_factor, mode_two_factor):
    flat_field = field.reshape(-1, N1)
    gram_raw = lax.dot_general(flat_field, flat_field, (((0,), (0,)), ((), ())), preferred_element_type=jnp.float32)
    gram_one = gram_raw * (1.0 / (V * N3 * N2))
    shrunk_flat = jnp.dot(flat_field, mode_one_factor, preferred_element_type=jnp.float32)
    shrunk = shrunk_flat.astype(jnp.bfloat16).reshape(V, N3, N2, R1)
    lines_two = jnp.transpose(shrunk, (2, 0, 1, 3)).reshape(N2, -1)
    gram_two_raw = lax.dot_general(lines_two, lines_two, (((1,), (1,)), ((), ())), preferred_element_type=jnp.float32)
    gram_two = gram_two_raw * (1.0 / (V * N3 * R1))
    moved = jnp.transpose(shrunk, (0, 1, 3, 2)).reshape(-1, N2)
    core_flat = jnp.dot(moved, mode_two_factor, preferred_element_type=jnp.float32)
    core = jnp.transpose(core_flat.reshape(V, N3, R1, R2), (0, 1, 3, 2)).astype(jnp.bfloat16)
    return gram_one, gram_two, core
```

```python
import jax
import jax.numpy as jnp
from jax import lax
from jax.sharding import PartitionSpec as P


def local(field, mode_one_factor, mode_two_factor):
    vars_all, cells_three, cells_two, cells_one = field.shape
    count_gx = lax.axis_size("gx")
    count_gy = lax.axis_size("gy")
    own_rows = vars_all // count_gx
    total_three = cells_three * lax.axis_size("gz")
    total_two = cells_two * count_gy
    rank_one = mode_one_factor.shape[1]
    rank_two = mode_two_factor.shape[1]
    own_ranks = rank_two // count_gy

    factor_one = lax.all_gather(mode_one_factor, "gx", axis=0, tiled=True)
    piece = lax.all_gather(field, "gx", axis=3, tiled=True)
    width = piece.shape[3]
    gram_block = lax.dot_general(
        field.reshape(-1, cells_one),
        piece.reshape(-1, width),
        (((0,), (0,)), ((), ())),
        preferred_element_type=jnp.float32,
    )
    gram_sum = lax.psum(lax.psum(gram_block, "gz"), "gy")
    gram_one = gram_sum * (1.0 / (vars_all * total_three * total_two))

    own_vars = lax.dynamic_slice_in_dim(piece, lax.axis_index("gx") * own_rows, own_rows, axis=0)
    shrunk = jnp.dot(
        own_vars.reshape(-1, width), factor_one, preferred_element_type=jnp.float32
    ).astype(jnp.bfloat16).reshape(own_rows, cells_three, cells_two, rank_one)

    shrunk_all = lax.all_gather(shrunk, "gy", axis=2, tiled=True)
    gram_two_block = jnp.einsum(
        "akjr,akqr->jq", shrunk, shrunk_all, preferred_element_type=jnp.float32
    )
    gram_two = lax.psum(gram_two_block, ("gx", "gz")) * (1.0 / (vars_all * total_three * rank_one))

    factor_two = lax.all_gather(mode_two_factor, "gy", axis=0, tiled=True)
    own_cols = lax.dynamic_slice_in_dim(factor_two, lax.axis_index("gy") * own_ranks, own_ranks, axis=1)
    core = jnp.einsum(
        "akjr,js->aksr", shrunk_all, own_cols, preferred_element_type=jnp.float32
    ).astype(jnp.bfloat16)
    return (gram_one, gram_two, core)


def solution(mesh):
    placed = (P(None, "gz", "gy", "gx"), P("gx", None), P("gy", None))
    return jax.shard_map(
        local,
        mesh=mesh,
        in_specs=placed,
        out_specs=(P("gx", None), P("gy", None), P("gx", "gz", "gy", None)),
        check_vma=False,
    )
```

```python
import jax
import jax.numpy as jnp
from jax import lax
from jax.sharding import PartitionSpec as P


def local(field, mode_one_factor, mode_two_factor):
    vars_all, cells_three, cells_two, cells_one = field.shape
    count_gx = lax.axis_size("gx")
    count_gy = lax.axis_size("gy")
    own_rows = vars_all // count_gx
    total_three = cells_three * lax.axis_size("gz")
    total_two = cells_two * count_gy
    rank_one = mode_one_factor.shape[1]
    rank_two = mode_two_factor.shape[1]
    own_ranks = rank_two // count_gy

    slab = cells_three * cells_two
    factor_slabs = -(-rank_one // slab)
    factor_t = jnp.pad(mode_one_factor.T, ((0, factor_slabs * slab - rank_one), (0, 0)))
    joined = jnp.concatenate(
        [field, factor_t.reshape(factor_slabs, cells_three, cells_two, cells_one)], axis=0
    )
    joined_all = lax.all_gather(joined, "gx", axis=3, tiled=True)
    piece = joined_all[:vars_all]
    width = piece.shape[3]
    factor_one_t = joined_all[vars_all:].reshape(factor_slabs * slab, width)[:rank_one]

    gram_block = lax.dot_general(
        field.reshape(-1, cells_one),
        piece.reshape(-1, width),
        (((0,), (0,)), ((), ())),
        preferred_element_type=jnp.float32,
    )

    own_vars = lax.dynamic_slice_in_dim(piece, lax.axis_index("gx") * own_rows, own_rows, axis=0)
    shrunk = lax.dot_general(
        own_vars.reshape(-1, width),
        factor_one_t,
        (((1,), (1,)), ((), ())),
        preferred_element_type=jnp.float32,
    ).astype(jnp.bfloat16).reshape(own_rows, cells_three, cells_two, rank_one)

    if rank_one == rank_two:
        extra = jnp.broadcast_to(mode_two_factor, (1, cells_three) + mode_two_factor.shape)
        both_all = lax.all_gather(jnp.concatenate([shrunk, extra], axis=0), "gy", axis=2, tiled=True)
        shrunk_all = both_all[:own_rows]
        factor_two = both_all[own_rows, 0]
    else:
        shrunk_all = lax.all_gather(shrunk, "gy", axis=2, tiled=True)
        factor_two = lax.all_gather(mode_two_factor, "gy", axis=0, tiled=True)

    gram_block, shrunk_all, factor_two = lax.optimization_barrier((gram_block, shrunk_all, factor_two))
    gram_sum = lax.psum(lax.psum(gram_block, "gz"), "gy")
    gram_one = gram_sum * (1.0 / (vars_all * total_three * total_two))

    gram_two_block = jnp.einsum(
        "akjr,akqr->jq", shrunk, shrunk_all, preferred_element_type=jnp.float32
    )
    gram_two = lax.psum(gram_two_block, ("gx", "gz")) * (1.0 / (vars_all * total_three * rank_one))

    own_cols = lax.dynamic_slice_in_dim(factor_two, lax.axis_index("gy") * own_ranks, own_ranks, axis=1)
    core = jnp.einsum(
        "akjr,js->aksr", shrunk_all, own_cols, preferred_element_type=jnp.float32
    ).astype(jnp.bfloat16)
    return (gram_one, gram_two, core)


def solution(mesh):
    placed = (P(None, "gz", "gy", "gx"), P("gx", None), P("gy", None))
    return jax.shard_map(
        local,
        mesh=mesh,
        in_specs=placed,
        out_specs=(P("gx", None), P("gy", None), P("gx", "gz", "gy", None)),
        check_vma=False,
    )
```

```python
import jax
import jax.numpy as jnp
from jax import lax
from jax.sharding import PartitionSpec as P


def local(field, mode_one_factor, mode_two_factor):
    vars_all, cells_three, cells_two, cells_one = field.shape
    count_gx = lax.axis_size("gx")
    count_gy = lax.axis_size("gy")
    own_rows = vars_all // count_gx
    total_three = cells_three * lax.axis_size("gz")
    total_two = cells_two * count_gy
    rank_one = mode_one_factor.shape[1]
    rank_two = mode_two_factor.shape[1]
    own_ranks = rank_two // count_gy

    slab = cells_three * cells_two
    factor_slabs = -(-rank_one // slab)
    factor_t = jnp.pad(mode_one_factor.T, ((0, factor_slabs * slab - rank_one), (0, 0)))
    joined = jnp.concatenate(
        [field, factor_t.reshape(factor_slabs, cells_three, cells_two, cells_one)], axis=0
    )
    joined_all = lax.all_gather(joined, "gx", axis=3, tiled=True)
    width = joined_all.shape[3]
    factor_one_t = joined_all[vars_all:].reshape(factor_slabs * slab, width)[:rank_one]

    local_rows = jnp.concatenate([field, jnp.zeros_like(joined[vars_all:])], axis=0)
    gram_block = lax.dot_general(
        local_rows.reshape(-1, cells_one),
        joined_all.reshape(-1, width),
        (((0,), (0,)), ((), ())),
        preferred_element_type=jnp.float32,
    )

    own_vars = lax.dynamic_slice_in_dim(joined_all, lax.axis_index("gx") * own_rows, own_rows, axis=0)
    shrunk = lax.dot_general(
        own_vars.reshape(-1, width),
        factor_one_t,
        (((1,), (1,)), ((), ())),
        preferred_element_type=jnp.float32,
    ).astype(jnp.bfloat16).reshape(own_rows, cells_three, cells_two, rank_one)

    if rank_one == rank_two:
        extra = jnp.broadcast_to(mode_two_factor, (1, cells_three) + mode_two_factor.shape)
        both = jnp.concatenate([shrunk, extra], axis=0)
    else:
        both = shrunk
    sent = jnp.broadcast_to(both[None], (count_gy,) + both.shape).reshape((-1,) + both.shape[1:])
    got = lax.all_to_all(sent, "gy", 0, 0, tiled=True).reshape((count_gy,) + both.shape)
    got = jnp.moveaxis(got, 0, 2).reshape(both.shape[:2] + (count_gy * cells_two, rank_one))
    shrunk_all = got[:own_rows]
    if rank_one == rank_two:
        factor_two = got[own_rows, 0]
    else:
        factor_two = lax.all_gather(mode_two_factor, "gy", axis=0, tiled=True)

    gram_block, shrunk = lax.optimization_barrier((gram_block, shrunk))
    gram_sum = lax.psum(lax.psum(gram_block, "gz"), "gy")
    gram_one = gram_sum * (1.0 / (vars_all * total_three * total_two))

    gram_two_block = jnp.einsum(
        "akjr,akqr->jq", shrunk, shrunk_all, preferred_element_type=jnp.float32
    )
    gram_two = lax.psum(gram_two_block, ("gx", "gz")) * (1.0 / (vars_all * total_three * rank_one))

    own_cols = lax.dynamic_slice_in_dim(factor_two, lax.axis_index("gy") * own_ranks, own_ranks, axis=1)
    core = jnp.einsum(
        "akjr,js->aksr", shrunk_all, own_cols, preferred_element_type=jnp.float32
    ).astype(jnp.bfloat16)
    return (gram_one, gram_two, core)


def solution(mesh):
    placed = (P(None, "gz", "gy", "gx"), P("gx", None), P("gy", None))
    return jax.shard_map(
        local,
        mesh=mesh,
        in_specs=placed,
        out_specs=(P("gx", None), P("gy", None), P("gx", "gz", "gy", None)),
        check_vma=False,
    )
```

```python
import jax
import jax.numpy as jnp
from jax import lax
from jax.sharding import PartitionSpec as P


def local(field, mode_one_factor, mode_two_factor):
    vars_all, cells_three, cells_two, cells_one = field.shape
    count_gx = lax.axis_size("gx")
    count_gy = lax.axis_size("gy")
    own_rows = vars_all // count_gx
    total_three = cells_three * lax.axis_size("gz")
    total_two = cells_two * count_gy
    rank_one = mode_one_factor.shape[1]
    rank_two = mode_two_factor.shape[1]
    own_ranks = rank_two // count_gy

    product = jnp.dot(
        field.reshape(-1, cells_one), mode_one_factor, preferred_element_type=jnp.float32
    )
    shrunk_sum = lax.psum_scatter(
        product.reshape(vars_all, cells_three, cells_two, rank_one),
        "gx",
        scatter_dimension=0,
        tiled=True,
    )
    field_later, shrunk_sum = lax.optimization_barrier((field, shrunk_sum))
    shrunk = shrunk_sum.astype(jnp.bfloat16)

    if rank_one == rank_two:
        extra = jnp.broadcast_to(mode_two_factor, (1, cells_three) + mode_two_factor.shape)
        both = jnp.concatenate([shrunk, extra], axis=0)
    else:
        both = shrunk
    sent = jnp.broadcast_to(both[None], (count_gy,) + both.shape).reshape((-1,) + both.shape[1:])
    got = lax.all_to_all(sent, "gy", 0, 0, tiled=True).reshape((count_gy,) + both.shape)

    piece = lax.all_gather(field_later, "gx", axis=3, tiled=True)
    width = piece.shape[3]
    gram_block = lax.dot_general(
        field_later.reshape(-1, cells_one),
        piece.reshape(-1, width),
        (((0,), (0,)), ((), ())),
        preferred_element_type=jnp.float32,
    )
    gram_block, got = lax.optimization_barrier((gram_block, got))
    gram_sum = lax.psum(lax.psum(gram_block, "gz"), "gy")
    gram_one = gram_sum * (1.0 / (vars_all * total_three * total_two))

    got = jnp.moveaxis(got, 0, 2).reshape(both.shape[:2] + (count_gy * cells_two, rank_one))
    shrunk_all = got[:own_rows]
    if rank_one == rank_two:
        factor_two = got[own_rows, 0]
    else:
        factor_two = lax.all_gather(mode_two_factor, "gy", axis=0, tiled=True)

    gram_two_block = jnp.einsum(
        "akjr,akqr->jq", shrunk, shrunk_all, preferred_element_type=jnp.float32
    )
    gram_two = lax.psum(gram_two_block, ("gx", "gz")) * (1.0 / (vars_all * total_three * rank_one))

    own_cols = lax.dynamic_slice_in_dim(factor_two, lax.axis_index("gy") * own_ranks, own_ranks, axis=1)
    core = jnp.einsum(
        "akjr,js->aksr", shrunk_all, own_cols, preferred_element_type=jnp.float32
    ).astype(jnp.bfloat16)
    return (gram_one, gram_two, core)


def solution(mesh):
    placed = (P(None, "gz", "gy", "gx"), P("gx", None), P("gy", None))
    return jax.shard_map(
        local,
        mesh=mesh,
        in_specs=placed,
        out_specs=(P("gx", None), P("gy", None), P("gx", "gz", "gy", None)),
        check_vma=False,
    )
```

```python
import jax
import jax.numpy as jnp
from jax import lax
from jax.sharding import PartitionSpec as P


def local(field, mode_one_factor, mode_two_factor):
    vars_all, cells_three, cells_two, cells_one = field.shape
    count_gx = lax.axis_size("gx")
    count_gy = lax.axis_size("gy")
    own_rows = vars_all // count_gx
    total_three = cells_three * lax.axis_size("gz")
    total_two = cells_two * count_gy
    rank_one = mode_one_factor.shape[1]
    rank_two = mode_two_factor.shape[1]
    own_ranks = rank_two // count_gy

    product = jnp.dot(
        field.reshape(-1, cells_one), mode_one_factor, preferred_element_type=jnp.float32
    )
    shrunk_sum = lax.psum_scatter(
        product.reshape(vars_all, cells_three, cells_two, rank_one),
        "gx",
        scatter_dimension=0,
        tiled=True,
    )
    field_later, shrunk_sum = lax.optimization_barrier((field, shrunk_sum))
    shrunk = shrunk_sum.astype(jnp.bfloat16)

    if rank_one == rank_two:
        extra = jnp.broadcast_to(mode_two_factor, (1, cells_three) + mode_two_factor.shape)
        both = jnp.concatenate([shrunk, extra], axis=0)
    else:
        both = shrunk
    sent = jnp.broadcast_to(both[None], (count_gy,) + both.shape).reshape((-1,) + both.shape[1:])
    got = lax.all_to_all(sent, "gy", 0, 0, tiled=True).reshape((count_gy,) + both.shape)

    piece = lax.all_gather(field_later, "gx", axis=3, tiled=True)
    width = piece.shape[3]
    gram_block = lax.dot_general(
        field_later.reshape(-1, cells_one),
        piece.reshape(-1, width),
        (((0,), (0,)), ((), ())),
        preferred_element_type=jnp.float32,
    )
    gram_block, got = lax.optimization_barrier((gram_block, got))
    got = jnp.moveaxis(got, 0, 2).reshape(both.shape[:2] + (count_gy * cells_two, rank_one))
    shrunk_all = got[:own_rows]
    if rank_one == rank_two:
        factor_two = got[own_rows, 0]
    else:
        factor_two = lax.all_gather(mode_two_factor, "gy", axis=0, tiled=True)

    gram_two_block = jnp.einsum(
        "akjr,akqr->jq", shrunk, shrunk_all, preferred_element_type=jnp.float32
    )
    two_size = gram_two_block.size
    extra_rows = -(-two_size // width)
    extra_rows = -(-extra_rows // 8) * 8
    two_rows = jnp.pad(gram_two_block.reshape(-1), (0, extra_rows * width - two_size))
    stacked = jnp.concatenate([gram_block, two_rows.reshape(extra_rows, width)], axis=0)
    stacked = lax.psum(stacked, "gz")
    own_gram = stacked.shape[0] - extra_rows
    gram_sum = lax.psum(stacked[:own_gram], "gy")
    gram_one = gram_sum * (1.0 / (vars_all * total_three * total_two))
    two_sum = stacked[own_gram:].reshape(-1)[:two_size].reshape(gram_two_block.shape)
    gram_two = lax.psum(two_sum, "gx") * (1.0 / (vars_all * total_three * rank_one))

    own_cols = lax.dynamic_slice_in_dim(factor_two, lax.axis_index("gy") * own_ranks, own_ranks, axis=1)
    core = jnp.einsum(
        "akjr,js->aksr", shrunk_all, own_cols, preferred_element_type=jnp.float32
    ).astype(jnp.bfloat16)
    return (gram_one, gram_two, core)


def solution(mesh):
    placed = (P(None, "gz", "gy", "gx"), P("gx", None), P("gy", None))
    return jax.shard_map(
        local,
        mesh=mesh,
        in_specs=placed,
        out_specs=(P("gx", None), P("gy", None), P("gx", "gz", "gy", None)),
        check_vma=False,
    )
```

```python
import jax
import jax.numpy as jnp
from jax import lax
from jax.sharding import PartitionSpec as P


def local(field, mode_one_factor, mode_two_factor):
    vars_all, cells_three, cells_two, cells_one = field.shape
    count_gx = lax.axis_size("gx")
    count_gy = lax.axis_size("gy")
    own_rows = vars_all // count_gx
    total_three = cells_three * lax.axis_size("gz")
    total_two = cells_two * count_gy
    rank_one = mode_one_factor.shape[1]
    rank_two = mode_two_factor.shape[1]
    own_ranks = rank_two // count_gy

    product = jnp.dot(
        field.reshape(-1, cells_one), mode_one_factor, preferred_element_type=jnp.float32
    )
    shrunk_sum = lax.psum_scatter(
        product.reshape(vars_all, cells_three, cells_two, rank_one),
        "gx",
        scatter_dimension=0,
        tiled=True,
    )
    field_later, shrunk_sum = lax.optimization_barrier((field, shrunk_sum))
    shrunk = shrunk_sum.astype(jnp.bfloat16)

    if rank_one == rank_two:
        extra = jnp.broadcast_to(mode_two_factor, (1, cells_three) + mode_two_factor.shape)
        both = jnp.concatenate([shrunk, extra], axis=0)
    else:
        both = shrunk
    sent = jnp.broadcast_to(both[None], (count_gy,) + both.shape).reshape((-1,) + both.shape[1:])
    got = lax.all_to_all(sent, "gy", 0, 0, tiled=True).reshape((count_gy,) + both.shape)

    piece = lax.all_gather(field_later, "gx", axis=3, tiled=True)
    width = piece.shape[3]
    gram_block = lax.dot_general(
        field_later.reshape(-1, cells_one),
        piece.reshape(-1, width),
        (((0,), (0,)), ((), ())),
        preferred_element_type=jnp.float32,
    )
    gram_block, got = lax.optimization_barrier((gram_block, got))
    slice_rows = gram_block.shape[0] // count_gy
    parts = lax.all_to_all(gram_block, "gy", 0, 0, tiled=True)
    own_slice = jnp.sum(parts.reshape(count_gy, slice_rows, width), axis=0)
    own_slice = lax.psum(own_slice, "gz")
    copies = jnp.broadcast_to(own_slice[None], (count_gy,) + own_slice.shape).reshape(-1, width)
    gram_sum = lax.all_to_all(copies, "gy", 0, 0, tiled=True)
    gram_one = gram_sum * (1.0 / (vars_all * total_three * total_two))

    got = jnp.moveaxis(got, 0, 2).reshape(both.shape[:2] + (count_gy * cells_two, rank_one))
    shrunk_all = got[:own_rows]
    if rank_one == rank_two:
        factor_two = got[own_rows, 0]
    else:
        factor_two = lax.all_gather(mode_two_factor, "gy", axis=0, tiled=True)

    gram_two_block = jnp.einsum(
        "akjr,akqr->jq", shrunk, shrunk_all, preferred_element_type=jnp.float32
    )
    gram_two = lax.psum(gram_two_block, ("gx", "gz")) * (1.0 / (vars_all * total_three * rank_one))

    own_cols = lax.dynamic_slice_in_dim(factor_two, lax.axis_index("gy") * own_ranks, own_ranks, axis=1)
    core = jnp.einsum(
        "akjr,js->aksr", shrunk_all, own_cols, preferred_element_type=jnp.float32
    ).astype(jnp.bfloat16)
    return (gram_one, gram_two, core)


def solution(mesh):
    placed = (P(None, "gz", "gy", "gx"), P("gx", None), P("gy", None))
    return jax.shard_map(
        local,
        mesh=mesh,
        in_specs=placed,
        out_specs=(P("gx", None), P("gy", None), P("gx", "gz", "gy", None)),
        check_vma=False,
    )
```

```python
import jax
import jax.numpy as jnp
from jax import lax
from jax.sharding import PartitionSpec as P


def local(field, mode_one_factor, mode_two_factor):
    vars_all, cells_three, cells_two, cells_one = field.shape
    count_gx = lax.axis_size("gx")
    count_gy = lax.axis_size("gy")
    own_rows = vars_all // count_gx
    total_three = cells_three * lax.axis_size("gz")
    total_two = cells_two * count_gy
    rank_one = mode_one_factor.shape[1]
    rank_two = mode_two_factor.shape[1]
    own_ranks = rank_two // count_gy

    product = jnp.dot(
        field.reshape(-1, cells_one), mode_one_factor, preferred_element_type=jnp.float32
    )
    shrunk_sum = lax.psum_scatter(
        product.reshape(vars_all, cells_three, cells_two, rank_one),
        "gx",
        scatter_dimension=0,
        tiled=True,
    )
    field_later, shrunk_sum = lax.optimization_barrier((field, shrunk_sum))
    shrunk = shrunk_sum.astype(jnp.bfloat16)

    if rank_one == rank_two:
        extra = jnp.broadcast_to(mode_two_factor, (1, cells_three) + mode_two_factor.shape)
        both = jnp.concatenate([shrunk, extra], axis=0)
    else:
        both = shrunk
    sent = jnp.broadcast_to(both[None], (count_gy,) + both.shape).reshape((-1,) + both.shape[1:])
    got = lax.all_to_all(sent, "gy", 0, 0, tiled=True).reshape((count_gy,) + both.shape)

    piece = lax.all_gather(field_later, "gx", axis=3, tiled=True)
    width = piece.shape[3]
    gram_block = lax.dot_general(
        field_later.reshape(-1, cells_one),
        piece.reshape(-1, width),
        (((0,), (0,)), ((), ())),
        preferred_element_type=jnp.float32,
    )
    gram_block, got = lax.optimization_barrier((gram_block, got))
    got = jnp.moveaxis(got, 0, 2).reshape(both.shape[:2] + (count_gy * cells_two, rank_one))
    shrunk_all = got[:own_rows]
    if rank_one == rank_two:
        factor_two = got[own_rows, 0]
    else:
        factor_two = lax.all_gather(mode_two_factor, "gy", axis=0, tiled=True)
    gram_two_block = jnp.einsum(
        "akjr,akqr->jq", shrunk, shrunk_all, preferred_element_type=jnp.float32
    )

    slice_rows = gram_block.shape[0] // count_gy
    parts = lax.all_to_all(gram_block, "gy", 0, 0, tiled=True)
    own_slice = jnp.sum(parts.reshape(count_gy, slice_rows, width), axis=0)
    two_size = gram_two_block.size
    extra_rows = -(-two_size // width)
    extra_rows = -(-extra_rows // 8) * 8
    two_rows = jnp.pad(gram_two_block.reshape(-1), (0, extra_rows * width - two_size))
    stacked = lax.psum(jnp.concatenate([own_slice, two_rows.reshape(extra_rows, width)], axis=0), "gz")
    own_slice = stacked[:slice_rows]
    copies = jnp.broadcast_to(own_slice[None], (count_gy,) + own_slice.shape).reshape(-1, width)
    gram_sum = lax.all_to_all(copies, "gy", 0, 0, tiled=True)
    gram_one = gram_sum * (1.0 / (vars_all * total_three * total_two))
    two_sum = stacked[slice_rows:].reshape(-1)[:two_size].reshape(gram_two_block.shape)
    gram_two = lax.psum(two_sum, "gx") * (1.0 / (vars_all * total_three * rank_one))

    own_cols = lax.dynamic_slice_in_dim(factor_two, lax.axis_index("gy") * own_ranks, own_ranks, axis=1)
    core = jnp.einsum(
        "akjr,js->aksr", shrunk_all, own_cols, preferred_element_type=jnp.float32
    ).astype(jnp.bfloat16)
    return (gram_one, gram_two, core)


def solution(mesh):
    placed = (P(None, "gz", "gy", "gx"), P("gx", None), P("gy", None))
    return jax.shard_map(
        local,
        mesh=mesh,
        in_specs=placed,
        out_specs=(P("gx", None), P("gy", None), P("gx", "gz", "gy", None)),
        check_vma=False,
    )
```

```python
import jax
import jax.numpy as jnp
from jax import lax
from jax.sharding import PartitionSpec as P


def local(field, mode_one_factor, mode_two_factor):
    vars_all, cells_three, cells_two, cells_one = field.shape
    count_gx = lax.axis_size("gx")
    count_gy = lax.axis_size("gy")
    own_rows = vars_all // count_gx
    total_three = cells_three * lax.axis_size("gz")
    total_two = cells_two * count_gy
    rank_one = mode_one_factor.shape[1]
    rank_two = mode_two_factor.shape[1]
    own_ranks = rank_two // count_gy

    product = jnp.dot(
        field.reshape(-1, cells_one), mode_one_factor, preferred_element_type=jnp.float32
    )
    shrunk_sum = lax.psum_scatter(
        product.reshape(vars_all, cells_three, cells_two, rank_one),
        "gx",
        scatter_dimension=0,
        tiled=True,
    )
    field_later, shrunk_sum = lax.optimization_barrier((field, shrunk_sum))
    shrunk = shrunk_sum.astype(jnp.bfloat16)

    if rank_one == rank_two:
        extra = jnp.broadcast_to(mode_two_factor, (1, cells_three) + mode_two_factor.shape)
        both = jnp.concatenate([shrunk, extra], axis=0)
    else:
        both = shrunk
    sent_early = jnp.broadcast_to(both[None], (count_gy,) + both.shape).reshape((-1,) + both.shape[1:])

    piece = lax.all_gather(field_later, "gx", axis=3, tiled=True)
    width = piece.shape[3]
    gram_block = lax.dot_general(
        field_later.reshape(-1, cells_one),
        piece.reshape(-1, width),
        (((0,), (0,)), ((), ())),
        preferred_element_type=jnp.float32,
    )
    sent, gram_block = lax.optimization_barrier((sent_early, gram_block))
    got = lax.all_to_all(sent, "gy", 0, 0, tiled=True).reshape((count_gy,) + both.shape)
    gram_block = lax.psum(gram_block, "gz")
    gram_block, got = lax.optimization_barrier((gram_block, got))

    slice_rows = gram_block.shape[0] // count_gy
    parts = lax.all_to_all(gram_block, "gy", 0, 0, tiled=True)
    own_slice = jnp.sum(parts.reshape(count_gy, slice_rows, width), axis=0)
    copies = jnp.broadcast_to(own_slice[None], (count_gy,) + own_slice.shape).reshape(-1, width)
    gram_sum = lax.all_to_all(copies, "gy", 0, 0, tiled=True)
    gram_one = gram_sum * (1.0 / (vars_all * total_three * total_two))

    got = jnp.moveaxis(got, 0, 2).reshape(both.shape[:2] + (count_gy * cells_two, rank_one))
    shrunk_all = got[:own_rows]
    if rank_one == rank_two:
        factor_two = got[own_rows, 0]
    else:
        factor_two = lax.all_gather(mode_two_factor, "gy", axis=0, tiled=True)
    gram_two_block = jnp.einsum(
        "akjr,akqr->jq", shrunk, shrunk_all, preferred_element_type=jnp.float32
    )
    gram_two = lax.psum(lax.psum(gram_two_block, "gx"), "gz") * (1.0 / (vars_all * total_three * rank_one))

    own_cols = lax.dynamic_slice_in_dim(factor_two, lax.axis_index("gy") * own_ranks, own_ranks, axis=1)
    core = jnp.einsum(
        "akjr,js->aksr", shrunk_all, own_cols, preferred_element_type=jnp.float32
    ).astype(jnp.bfloat16)
    return (gram_one, gram_two, core)


def solution(mesh):
    placed = (P(None, "gz", "gy", "gx"), P("gx", None), P("gy", None))
    return jax.shard_map(
        local,
        mesh=mesh,
        in_specs=placed,
        out_specs=(P("gx", None), P("gy", None), P("gx", "gz", "gy", None)),
        check_vma=False,
    )
```

```python
import jax
import jax.numpy as jnp
from jax import lax
from jax.sharding import PartitionSpec as P


def local(field, mode_one_factor, mode_two_factor):
    vars_all, cells_three, cells_two, cells_one = field.shape
    count_gx = lax.axis_size("gx")
    count_gy = lax.axis_size("gy")
    own_rows = vars_all // count_gx
    total_three = cells_three * lax.axis_size("gz")
    total_two = cells_two * count_gy
    rank_one = mode_one_factor.shape[1]
    rank_two = mode_two_factor.shape[1]
    own_ranks = rank_two // count_gy

    product = jnp.dot(
        field.reshape(-1, cells_one), mode_one_factor, preferred_element_type=jnp.float32
    )
    shrunk_sum = lax.psum_scatter(
        product.reshape(vars_all, cells_three, cells_two, rank_one),
        "gx",
        scatter_dimension=0,
        tiled=True,
    )
    field_later, shrunk_sum = lax.optimization_barrier((field, shrunk_sum))
    shrunk = shrunk_sum.astype(jnp.bfloat16)

    if rank_one == rank_two:
        extra = jnp.broadcast_to(mode_two_factor, (1, cells_three) + mode_two_factor.shape)
        both = jnp.concatenate([shrunk, extra], axis=0)
    else:
        both = shrunk
    sent = jnp.broadcast_to(both[None], (count_gy,) + both.shape).reshape((-1,) + both.shape[1:])
    got = lax.all_to_all(sent, "gy", 0, 0, tiled=True).reshape((count_gy,) + both.shape)

    piece = lax.all_gather(field_later, "gx", axis=3, tiled=True)
    width = piece.shape[3]
    gram_block = lax.dot_general(
        field_later.reshape(-1, cells_one),
        piece.reshape(-1, width),
        (((0,), (0,)), ((), ())),
        preferred_element_type=jnp.float32,
    )
    gram_block, got = lax.optimization_barrier((gram_block, got))
    got = jnp.moveaxis(got, 0, 2).reshape(both.shape[:2] + (count_gy * cells_two, rank_one))
    shrunk_all = got[:own_rows]
    if rank_one == rank_two:
        factor_two = got[own_rows, 0]
    else:
        factor_two = lax.all_gather(mode_two_factor, "gy", axis=0, tiled=True)
    gram_two_block = jnp.einsum(
        "akjr,akqr->jq", shrunk, shrunk_all, preferred_element_type=jnp.float32
    )

    slice_rows = gram_block.shape[0] // count_gy
    parts = lax.all_to_all(gram_block, "gy", 0, 0, tiled=True)
    own_slice = jnp.sum(parts.reshape(count_gy, slice_rows, width), axis=0)
    two_size = gram_two_block.size
    extra_rows = -(-two_size // width)
    extra_rows = -(-extra_rows // 8) * 8
    two_rows = jnp.pad(gram_two_block.reshape(-1), (0, extra_rows * width - two_size))
    stacked = jnp.concatenate([own_slice, two_rows.reshape(extra_rows, width)], axis=0)
    count_gz = lax.axis_size("gz")
    chunk = -(-stacked.shape[0] // (8 * count_gz)) * 8
    stacked = jnp.pad(stacked, ((0, chunk * count_gz - stacked.shape[0]), (0, 0)))
    pieces = lax.all_to_all(stacked, "gz", 0, 0, tiled=True)
    own_chunk = jnp.sum(pieces.reshape(count_gz, chunk, width), axis=0)
    chunk_copies = jnp.broadcast_to(own_chunk[None], (count_gz,) + own_chunk.shape).reshape(-1, width)
    stacked = lax.all_to_all(chunk_copies, "gz", 0, 0, tiled=True)
    own_slice = stacked[:slice_rows]
    copies = jnp.broadcast_to(own_slice[None], (count_gy,) + own_slice.shape).reshape(-1, width)
    gram_sum = lax.all_to_all(copies, "gy", 0, 0, tiled=True)
    gram_one = gram_sum * (1.0 / (vars_all * total_three * total_two))
    two_sum = stacked[slice_rows:].reshape(-1)[:two_size].reshape(gram_two_block.shape)
    gram_two = lax.psum(two_sum, "gx") * (1.0 / (vars_all * total_three * rank_one))

    own_cols = lax.dynamic_slice_in_dim(factor_two, lax.axis_index("gy") * own_ranks, own_ranks, axis=1)
    core = jnp.einsum(
        "akjr,js->aksr", shrunk_all, own_cols, preferred_element_type=jnp.float32
    ).astype(jnp.bfloat16)
    return (gram_one, gram_two, core)


def solution(mesh):
    placed = (P(None, "gz", "gy", "gx"), P("gx", None), P("gy", None))
    return jax.shard_map(
        local,
        mesh=mesh,
        in_specs=placed,
        out_specs=(P("gx", None), P("gy", None), P("gx", "gz", "gy", None)),
        check_vma=False,
    )
```

```python
import jax
import jax.numpy as jnp
from jax import lax
from jax.sharding import PartitionSpec as P


def local(field, mode_one_factor, mode_two_factor):
    vars_all, cells_three, cells_two, cells_one = field.shape
    count_gx = lax.axis_size("gx")
    count_gy = lax.axis_size("gy")
    own_rows = vars_all // count_gx
    total_three = cells_three * lax.axis_size("gz")
    total_two = cells_two * count_gy
    rank_one = mode_one_factor.shape[1]
    rank_two = mode_two_factor.shape[1]
    own_ranks = rank_two // count_gy

    product = jnp.dot(
        field.reshape(-1, cells_one), mode_one_factor, preferred_element_type=jnp.float32
    )
    shrunk_parts = lax.all_to_all(
        product.reshape(vars_all, cells_three, cells_two, rank_one), "gx", 0, 0, tiled=True
    )
    shrunk_sum = jnp.sum(
        shrunk_parts.reshape((count_gx, own_rows) + shrunk_parts.shape[1:]), axis=0
    )
    shrunk = shrunk_sum.astype(jnp.bfloat16)

    if rank_one == rank_two:
        extra = jnp.broadcast_to(mode_two_factor, (1, cells_three) + mode_two_factor.shape)
        both = jnp.concatenate([shrunk, extra], axis=0)
    else:
        both = shrunk
    sent = jnp.broadcast_to(both[None], (count_gy,) + both.shape).reshape((-1,) + both.shape[1:])
    got = lax.all_to_all(sent, "gy", 0, 0, tiled=True).reshape((count_gy,) + both.shape)

    piece = lax.all_gather(field, "gx", axis=3, tiled=True)
    width = piece.shape[3]
    gram_block = lax.dot_general(
        field.reshape(-1, cells_one),
        piece.reshape(-1, width),
        (((0,), (0,)), ((), ())),
        preferred_element_type=jnp.float32,
    )
    gram_block, got = lax.optimization_barrier((gram_block, got))
    got = jnp.moveaxis(got, 0, 2).reshape(both.shape[:2] + (count_gy * cells_two, rank_one))
    shrunk_all = got[:own_rows]
    if rank_one == rank_two:
        factor_two = got[own_rows, 0]
    else:
        factor_two = lax.all_gather(mode_two_factor, "gy", axis=0, tiled=True)
    gram_two_block = jnp.einsum(
        "akjr,akqr->jq", shrunk, shrunk_all, preferred_element_type=jnp.float32
    )

    slice_rows = gram_block.shape[0] // count_gy
    parts = lax.all_to_all(gram_block, "gy", 0, 0, tiled=True)
    own_slice = jnp.sum(parts.reshape(count_gy, slice_rows, width), axis=0)
    two_size = gram_two_block.size
    extra_rows = -(-two_size // width)
    extra_rows = -(-extra_rows // 8) * 8
    two_rows = jnp.pad(gram_two_block.reshape(-1), (0, extra_rows * width - two_size))
    stacked = jnp.concatenate([own_slice, two_rows.reshape(extra_rows, width)], axis=0)
    count_gz = lax.axis_size("gz")
    chunk = -(-stacked.shape[0] // (8 * count_gz)) * 8
    stacked = jnp.pad(stacked, ((0, chunk * count_gz - stacked.shape[0]), (0, 0)))
    pieces = lax.all_to_all(stacked, "gz", 0, 0, tiled=True)
    own_chunk = jnp.sum(pieces.reshape(count_gz, chunk, width), axis=0)
    chunk_copies = jnp.broadcast_to(own_chunk[None], (count_gz,) + own_chunk.shape).reshape(-1, width)
    stacked = lax.all_to_all(chunk_copies, "gz", 0, 0, tiled=True)
    own_slice = stacked[:slice_rows]
    copies = jnp.broadcast_to(own_slice[None], (count_gy,) + own_slice.shape).reshape(-1, width)
    gram_sum = lax.all_to_all(copies, "gy", 0, 0, tiled=True)
    gram_one = gram_sum * (1.0 / (vars_all * total_three * total_two))
    two_sum = stacked[slice_rows:].reshape(-1)[:two_size].reshape(gram_two_block.shape)
    gram_two = lax.psum(two_sum, "gx") * (1.0 / (vars_all * total_three * rank_one))

    own_cols = lax.dynamic_slice_in_dim(factor_two, lax.axis_index("gy") * own_ranks, own_ranks, axis=1)
    core = jnp.einsum(
        "akjr,js->aksr", shrunk_all, own_cols, preferred_element_type=jnp.float32
    ).astype(jnp.bfloat16)
    return (gram_one, gram_two, core)


def solution(mesh):
    placed = (P(None, "gz", "gy", "gx"), P("gx", None), P("gy", None))
    return jax.shard_map(
        local,
        mesh=mesh,
        in_specs=placed,
        out_specs=(P("gx", None), P("gy", None), P("gx", "gz", "gy", None)),
        check_vma=False,
    )
```

```python
import jax
import jax.numpy as jnp
from jax import lax
from jax.sharding import PartitionSpec as P


def local(field, mode_one_factor, mode_two_factor):
    vars_all, cells_three, cells_two, cells_one = field.shape
    count_gx = lax.axis_size("gx")
    count_gy = lax.axis_size("gy")
    own_rows = vars_all // count_gx
    total_three = cells_three * lax.axis_size("gz")
    total_two = cells_two * count_gy
    rank_one = mode_one_factor.shape[1]
    rank_two = mode_two_factor.shape[1]
    own_ranks = rank_two // count_gy

    product = jnp.dot(
        field.reshape(-1, cells_one), mode_one_factor, preferred_element_type=jnp.float32
    )
    shrunk_sum = lax.psum_scatter(
        product.reshape(vars_all, cells_three, cells_two, rank_one),
        "gx",
        scatter_dimension=0,
        tiled=True,
    )
    field_later, shrunk_sum = lax.optimization_barrier((field, shrunk_sum))
    shrunk = shrunk_sum.astype(jnp.bfloat16)

    if rank_one == rank_two:
        extra = jnp.broadcast_to(mode_two_factor, (1, cells_three) + mode_two_factor.shape)
        both = jnp.concatenate([shrunk, extra], axis=0)
    else:
        both = shrunk
    sent = jnp.broadcast_to(both[None], (count_gy,) + both.shape).reshape((-1,) + both.shape[1:])
    got = lax.all_to_all(sent, "gy", 0, 0, tiled=True).reshape((count_gy,) + both.shape)

    piece = lax.all_gather(field_later, "gx", axis=3, tiled=True)
    width = piece.shape[3]
    gram_block = lax.dot_general(
        field_later.reshape(-1, cells_one),
        piece.reshape(-1, width),
        (((0,), (0,)), ((), ())),
        preferred_element_type=jnp.float32,
    )
    gram_block, got = lax.optimization_barrier((gram_block, got))
    got = jnp.moveaxis(got, 0, 2).reshape(both.shape[:2] + (count_gy * cells_two, rank_one))
    shrunk_all = got[:own_rows]
    if rank_one == rank_two:
        factor_two = got[own_rows, 0]
    else:
        factor_two = lax.all_gather(mode_two_factor, "gy", axis=0, tiled=True)
    gram_two_block = jnp.einsum(
        "akjr,akqr->jq", shrunk, shrunk_all, preferred_element_type=jnp.float32
    )

    slice_rows = gram_block.shape[0] // count_gy
    parts = lax.all_to_all(gram_block, "gy", 0, 0, tiled=True)
    own_slice = jnp.sum(parts.reshape(count_gy, slice_rows, width), axis=0)
    two_size = gram_two_block.size
    extra_rows = -(-two_size // width)
    extra_rows = -(-extra_rows // 8) * 8
    two_rows = jnp.pad(gram_two_block.reshape(-1), (0, extra_rows * width - two_size))
    stacked = jnp.concatenate([own_slice, two_rows.reshape(extra_rows, width)], axis=0)
    count_gz = lax.axis_size("gz")
    gz_copies = jnp.broadcast_to(stacked[None], (count_gz,) + stacked.shape).reshape(-1, width)
    gz_blocks = lax.all_to_all(gz_copies, "gz", 0, 0, tiled=True)
    stacked = jnp.sum(gz_blocks.reshape((count_gz,) + stacked.shape), axis=0)
    own_slice = stacked[:slice_rows]
    copies = jnp.broadcast_to(own_slice[None], (count_gy,) + own_slice.shape).reshape(-1, width)
    gram_sum = lax.all_to_all(copies, "gy", 0, 0, tiled=True)
    gram_one = gram_sum * (1.0 / (vars_all * total_three * total_two))
    two_sum = stacked[slice_rows:].reshape(-1)[:two_size].reshape(gram_two_block.shape)
    gram_two = lax.psum(two_sum, "gx") * (1.0 / (vars_all * total_three * rank_one))

    own_cols = lax.dynamic_slice_in_dim(factor_two, lax.axis_index("gy") * own_ranks, own_ranks, axis=1)
    core = jnp.einsum(
        "akjr,js->aksr", shrunk_all, own_cols, preferred_element_type=jnp.float32
    ).astype(jnp.bfloat16)
    return (gram_one, gram_two, core)


def solution(mesh):
    placed = (P(None, "gz", "gy", "gx"), P("gx", None), P("gy", None))
    return jax.shard_map(
        local,
        mesh=mesh,
        in_specs=placed,
        out_specs=(P("gx", None), P("gy", None), P("gx", "gz", "gy", None)),
        check_vma=False,
    )
```

```python
import jax
import jax.numpy as jnp
from jax import lax
from jax.sharding import PartitionSpec as P


def local(field, mode_one_factor, mode_two_factor):
    vars_all, cells_three, cells_two, cells_one = field.shape
    count_gx = lax.axis_size("gx")
    count_gy = lax.axis_size("gy")
    own_rows = vars_all // count_gx
    total_three = cells_three * lax.axis_size("gz")
    total_two = cells_two * count_gy
    rank_one = mode_one_factor.shape[1]
    rank_two = mode_two_factor.shape[1]
    own_ranks = rank_two // count_gy

    product = jnp.dot(
        field.reshape(-1, cells_one), mode_one_factor, preferred_element_type=jnp.float32
    )
    shrunk_sum = lax.psum_scatter(
        product.reshape(vars_all, cells_three, cells_two, rank_one),
        "gx",
        scatter_dimension=0,
        tiled=True,
    )
    field_later, shrunk_sum = lax.optimization_barrier((field, shrunk_sum))
    shrunk = shrunk_sum.astype(jnp.bfloat16)

    if rank_one == rank_two:
        extra = jnp.broadcast_to(mode_two_factor, (1, cells_three) + mode_two_factor.shape)
        both = jnp.concatenate([shrunk, extra], axis=0)
    else:
        both = shrunk
    sent = jnp.broadcast_to(both[None], (count_gy,) + both.shape).reshape((-1,) + both.shape[1:])
    got = lax.all_to_all(sent, "gy", 0, 0, tiled=True).reshape((count_gy,) + both.shape)

    piece = lax.all_gather(field_later, "gx", axis=3, tiled=True)
    width = piece.shape[3]
    gram_block = lax.dot_general(
        field_later.reshape(-1, cells_one),
        piece.reshape(-1, width),
        (((0,), (0,)), ((), ())),
        preferred_element_type=jnp.float32,
    )
    gram_block, got = lax.optimization_barrier((gram_block, got))
    got = jnp.moveaxis(got, 0, 2).reshape(both.shape[:2] + (count_gy * cells_two, rank_one))
    shrunk_all = got[:own_rows]
    if rank_one == rank_two:
        factor_two = got[own_rows, 0]
    else:
        factor_two = lax.all_gather(mode_two_factor, "gy", axis=0, tiled=True)
    gram_two_block = jnp.einsum(
        "akjr,akqr->jq", shrunk, shrunk_all, preferred_element_type=jnp.float32
    )

    slice_rows = gram_block.shape[0] // count_gy
    parts = lax.all_to_all(gram_block.astype(jnp.bfloat16), "gy", 0, 0, tiled=True)
    own_slice = jnp.sum(parts.reshape(count_gy, slice_rows, width).astype(jnp.float32), axis=0)
    two_size = gram_two_block.size
    extra_rows = -(-two_size // width)
    extra_rows = -(-extra_rows // 8) * 8
    two_rows = jnp.pad(gram_two_block.reshape(-1), (0, extra_rows * width - two_size))
    stacked = jnp.concatenate([own_slice, two_rows.reshape(extra_rows, width)], axis=0)
    count_gz = lax.axis_size("gz")
    gz_copies = jnp.broadcast_to(stacked[None], (count_gz,) + stacked.shape).reshape(-1, width)
    gz_blocks = lax.all_to_all(gz_copies, "gz", 0, 0, tiled=True)
    stacked = jnp.sum(gz_blocks.reshape((count_gz,) + stacked.shape), axis=0)
    own_slice = stacked[:slice_rows]
    copies = jnp.broadcast_to(own_slice[None], (count_gy,) + own_slice.shape).reshape(-1, width)
    gram_sum = lax.all_to_all(copies, "gy", 0, 0, tiled=True)
    gram_one = gram_sum * (1.0 / (vars_all * total_three * total_two))
    two_sum = stacked[slice_rows:].reshape(-1)[:two_size].reshape(gram_two_block.shape)
    gram_two = lax.psum(two_sum, "gx") * (1.0 / (vars_all * total_three * rank_one))

    own_cols = lax.dynamic_slice_in_dim(factor_two, lax.axis_index("gy") * own_ranks, own_ranks, axis=1)
    core = jnp.einsum(
        "akjr,js->aksr", shrunk_all, own_cols, preferred_element_type=jnp.float32
    ).astype(jnp.bfloat16)
    return (gram_one, gram_two, core)


def solution(mesh):
    placed = (P(None, "gz", "gy", "gx"), P("gx", None), P("gy", None))
    return jax.shard_map(
        local,
        mesh=mesh,
        in_specs=placed,
        out_specs=(P("gx", None), P("gy", None), P("gx", "gz", "gy", None)),
        check_vma=False,
    )
```

```python
import jax
import jax.numpy as jnp
from jax import lax
from jax.sharding import PartitionSpec as P


def local(field, mode_one_factor, mode_two_factor):
    vars_all, cells_three, cells_two, cells_one = field.shape
    count_gx = lax.axis_size("gx")
    count_gy = lax.axis_size("gy")
    own_rows = vars_all // count_gx
    total_three = cells_three * lax.axis_size("gz")
    total_two = cells_two * count_gy
    rank_one = mode_one_factor.shape[1]
    rank_two = mode_two_factor.shape[1]
    own_ranks = rank_two // count_gy

    product = jnp.dot(
        field.reshape(-1, cells_one), mode_one_factor, preferred_element_type=jnp.float32
    )
    shrunk_sum = lax.psum_scatter(
        product.reshape(vars_all, cells_three, cells_two, rank_one),
        "gx",
        scatter_dimension=0,
        tiled=True,
    )
    field_later, shrunk_sum = lax.optimization_barrier((field, shrunk_sum))
    shrunk = shrunk_sum.astype(jnp.bfloat16)

    if rank_one == rank_two:
        extra = jnp.broadcast_to(mode_two_factor, (1, cells_three) + mode_two_factor.shape)
        both = jnp.concatenate([shrunk, extra], axis=0)
    else:
        both = shrunk
    sent = jnp.broadcast_to(both[None], (count_gy,) + both.shape).reshape((-1,) + both.shape[1:])
    got = lax.all_to_all(sent, "gy", 0, 0, tiled=True).reshape((count_gy,) + both.shape)

    piece = lax.all_gather(field_later, "gx", axis=3, tiled=True)
    width = piece.shape[3]
    gram_block = lax.dot_general(
        field_later.reshape(-1, cells_one),
        piece.reshape(-1, width),
        (((0,), (0,)), ((), ())),
        preferred_element_type=jnp.float32,
    )
    gram_block, got = lax.optimization_barrier((gram_block, got))
    got = jnp.moveaxis(got, 0, 2).reshape(both.shape[:2] + (count_gy * cells_two, rank_one))
    shrunk_all = got[:own_rows]
    if rank_one == rank_two:
        factor_two = got[own_rows, 0]
    else:
        factor_two = lax.all_gather(mode_two_factor, "gy", axis=0, tiled=True)
    gram_two_block = jnp.einsum(
        "akjr,akqr->jq", shrunk, shrunk_all, preferred_element_type=jnp.float32
    )

    slice_rows = gram_block.shape[0] // count_gy
    parts = lax.all_to_all(gram_block.astype(jnp.bfloat16), "gy", 0, 0, tiled=True)
    own_slice = jnp.sum(parts.reshape(count_gy, slice_rows, width).astype(jnp.float32), axis=0)
    two_size = gram_two_block.size
    extra_rows = -(-two_size // width)
    extra_rows = -(-extra_rows // 8) * 8
    two_rows = jnp.pad(gram_two_block.reshape(-1), (0, extra_rows * width - two_size))
    stacked = jnp.concatenate([own_slice, two_rows.reshape(extra_rows, width)], axis=0)
    count_gz = lax.axis_size("gz")
    gz_copies = jnp.broadcast_to(stacked[None], (count_gz,) + stacked.shape).reshape(-1, width)
    gz_blocks = lax.all_to_all(gz_copies, "gz", 0, 0, tiled=True)
    stacked = jnp.sum(gz_blocks.reshape((count_gz,) + stacked.shape), axis=0)
    own_slice = stacked[:slice_rows]
    copies = jnp.broadcast_to(own_slice[None], (count_gy,) + own_slice.shape).reshape(-1, width)
    gram_sum = lax.all_to_all(copies.astype(jnp.bfloat16), "gy", 0, 0, tiled=True).astype(jnp.float32)
    gram_one = gram_sum * (1.0 / (vars_all * total_three * total_two))
    two_sum = stacked[slice_rows:].reshape(-1)[:two_size].reshape(gram_two_block.shape)
    gram_two = lax.psum(two_sum, "gx") * (1.0 / (vars_all * total_three * rank_one))

    own_cols = lax.dynamic_slice_in_dim(factor_two, lax.axis_index("gy") * own_ranks, own_ranks, axis=1)
    core = jnp.einsum(
        "akjr,js->aksr", shrunk_all, own_cols, preferred_element_type=jnp.float32
    ).astype(jnp.bfloat16)
    return (gram_one, gram_two, core)


def solution(mesh):
    placed = (P(None, "gz", "gy", "gx"), P("gx", None), P("gy", None))
    return jax.shard_map(
        local,
        mesh=mesh,
        in_specs=placed,
        out_specs=(P("gx", None), P("gy", None), P("gx", "gz", "gy", None)),
        check_vma=False,
    )
```
